256 devices in a mesh: vir: 64 (over y, z, core), occ: 4 (over x).
Axes of the slice: x: 4, y: 4, z: 8, core: 2. Of those that a mesh axis runs over, the one named last changes fastest.
Arguments:
- tiles: float32 [4096, 128, 128], P('vir'), may hold values from -0.02734375 to 0.02734375
- tile_slot: int32 [4096], P('vir'), may hold values from 0 to 256, as said below
- amplitudes: float32 [262144, 1024], P('vir', 'occ'), may hold values from -6 to 6
- occ_energy: float32 [32], replicated, may hold values from -2 to -0.5
- vir_energy: float32 [32], replicated, may hold values from 0.5 to 3
Outputs:
- update: float32 [1024, 1024], P('vir', 'occ')
The draws below stay inside these ranges and needn't reach their ends.
Inputs may be any that keep to these rules, and one draw needn't show every extreme that they name: `tile_slot`: for each index v of vir, the slots v * 64 to v * 64 + 63 name distinct block positions below 256, live slots first, then the empty value 8 * 32; each index has 16 or more live slots and some index has all 64 live.
All inputs are finite; a program needn't handle non-finite values.
Results may differ from the reference program's by a relative error of at most 0.0003.
Values sent between devices are 32-bit elements; how exact they have to be, the bound alone decides.
No kernel may reach another device: no remote copies, remote signals or barrier semaphores. Data moves between devices by JAX's collectives and lax.ppermute only.
A program may use at most 64 MiB of HBM per device.

```python
import jax
import jax.numpy as jnp
from jax import lax

NV = 512
NO = 32
NW = 32
TILE = 128
NVP = 262144
NOP = 1024
ROW_BLOCKS = 8
COL_BLOCKS = 32
CAP = 64
N_VIR = 64


def draw_tile_slot(key, part):
    total_tiles = ROW_BLOCKS * COL_BLOCKS
    keys = jax.random.split(jax.random.fold_in(key, 11), N_VIR)

    def one_order(sub_key):
        return jax.random.permutation(sub_key, total_tiles)[:CAP]
    orders = jax.vmap(one_order)(keys)
    counts = jax.random.randint(jax.random.fold_in(key, 12), (N_VIR,), CAP // 4, CAP + 1)
    fullest = jax.random.randint(jax.random.fold_in(key, 13), (), 0, N_VIR)
    counts = jnp.where(jnp.arange(N_VIR) == fullest, CAP, counts)
    live = jnp.arange(CAP)[None, :] < counts[:, None]
    return jnp.where(live, orders, total_tiles).astype(jnp.int32).reshape(N_VIR * CAP)


def steps_of(own_key, extent, cuts, least, high):
    loudness = 1.0
    for position, parts in cuts:
        heights = jax.random.uniform(jax.random.fold_in(jax.random.fold_in(own_key, 6), position), (parts,), jnp.float32, least / len(cuts), high / len(cuts))
        loudness = loudness * jnp.repeat(jnp.exp(heights), extent[position] // parts).reshape((-1,) + (1,) * (len(extent) - 1 - position))
    return loudness


def noise(rng, dims, width, most, pieces=(), dtype=jnp.bfloat16):
    values = jax.random.normal(rng, dims, jnp.float32) * width
    if len(pieces) > 0:
        values = steps_of(rng, dims, pieces, -0.22, 0.18) * values
    return jnp.clip(values, min=-most, max=most).astype(dtype)


def setup_inputs(seed: int = 0) -> dict:
    streams_of = jax.random.split(jax.random.key(seed), 6)
    tiles = noise(streams_of[0], (N_VIR * CAP, TILE, TILE), (NV * NV // 5) ** -0.5, 0.02734375, ((0, 64),), jnp.float32)
    tile_slot = draw_tile_slot(jax.random.fold_in(streams_of[5], 71), 0)
    amplitudes = noise(streams_of[2], (NVP, NOP), 1.0, 6.0, ((0, 64), (1, 4)), jnp.float32)
    occ_energy = jnp.clip(jax.random.uniform(streams_of[3], (NO,), jnp.float32, -2.0, -0.5), -2.0, -0.5)
    vir_energy = jnp.clip(jax.random.uniform(streams_of[4], (NW,), jnp.float32, 0.5, 3.0), 0.5, 3.0)
    return dict(tiles=tiles, tile_slot=tile_slot, amplitudes=amplitudes, occ_energy=occ_energy, vir_energy=vir_energy)


def reference(tiles, tile_slot, amplitudes, occ_energy, vir_energy):
    row_blocks = NW * NW // TILE
    col_blocks = NV * NV // (N_VIR * TILE)
    pair_count = NO * NO
    tile_sets = tiles.reshape(N_VIR, CAP, TILE, TILE)
    slot_sets = tile_slot.reshape(N_VIR, CAP)
    amp_sets = amplitudes.reshape(N_VIR, col_blocks, TILE, pair_count)

    def add_device(running_sum, inputs):
        tile_set, slots, amp_block = inputs
        row_ids = (slots // col_blocks).astype(jnp.int32)
        col_ids = (slots % col_blocks).astype(jnp.int32)
        picked = amp_block[col_ids]
        products = jnp.einsum("kxy,kyn->kxn", tile_set, picked, precision=lax.Precision.HIGHEST)
        summed = jax.ops.segment_sum(products, row_ids, num_segments=row_blocks + 1)
        return running_sum + summed[:row_blocks], None

    start = jnp.zeros((row_blocks, TILE, pair_count), jnp.float32)
    ladder, unused = lax.scan(add_device, start, (tile_sets, slot_sets, amp_sets))
    pair_sums = ladder.reshape(NW, NW, NO, NO)
    mirror = pair_sums.transpose(1, 0, 3, 2)
    denominator = (occ_energy[None, None, :, None] + occ_energy[None, None, None, :]
                   - vir_energy[:, None, None, None] - vir_energy[None, :, None, None])
    return ((pair_sums + mirror) / denominator).reshape(NW * NW, NO * NO)
```

```python
import functools

import jax
import jax.numpy as jnp
from jax import lax
from jax.experimental import pallas as pl
from jax.experimental.pallas import tpu as pltpu
from jax.sharding import Mesh
from jax.sharding import PartitionSpec as P

F32 = jnp.float32
BF16 = jnp.bfloat16
TILE = 128
CAP = 64
COLS = 32
CHUNKS = 8
NY, NZ, NX = 4, 8, 4
HALF = 16
VIR = ("y", "z", "core")


def vmem_spec():
    return pl.BlockSpec(memory_space=pltpu.VMEM)


def split3(x):
    top = x.astype(BF16)
    rest = x - top.astype(F32)
    mid = rest.astype(BF16)
    low = (rest - mid.astype(F32)).astype(BF16)
    return top, mid, low


def permute_lanes(x, place):
    top, mid, low = split3(x)
    out = jnp.dot(low, place, preferred_element_type=F32)
    out = out + jnp.dot(mid, place, preferred_element_type=F32)
    return out + jnp.dot(top, place, preferred_element_type=F32)


def ladder_kernel(slot_ref, pos_ref, tiles_hbm, amps_hbm, keep_ref, send_ref, tbuf, abuf, stack, acc, tsem, asem):
    arows, trows = abuf.shape[0] // CHUNKS, CAP // CHUNKS

    def amp_copy(c):
        rows = pl.ds(c * arows, arows)
        return pltpu.make_async_copy(amps_hbm.at[rows], abuf.at[rows], asem.at[c])

    def tile_copy(c):
        rows = pl.ds(c * trows, trows)
        return pltpu.make_async_copy(tiles_hbm.at[rows], tbuf.at[rows], tsem.at[c])

    for c in range(CHUNKS):
        amp_copy(c).start()
    for c in range(CHUNKS):
        tile_copy(c).start()
    acc[...] = jnp.zeros_like(acc)
    for c in range(CHUNKS):
        amp_copy(c).wait()

        @pl.loop(0, arows // TILE)
        def _(q, c=c):
            block = c * (arows // TILE) + q
            a = abuf[pl.ds(pl.multiple_of(block * TILE, TILE), TILE), :]
            top = a.astype(BF16)
            stack[block, 0:TILE, :] = top
            stack[block, TILE : 2 * TILE, :] = (a - top.astype(F32)).astype(BF16)

    @pl.loop(0, CHUNKS)
    def _(c):
        tile_copy(c).wait()
        for u in range(trows):
            slot = slot_ref[c * trows + u]
            row = pl.multiple_of((slot // COLS) * TILE, TILE)
            col = slot % COLS
            t = tbuf[c * trows + u]
            top = t.astype(BF16)
            low = (t - top.astype(F32)).astype(BF16)
            part = jnp.dot(jnp.concatenate([top, top], axis=1), stack[col], preferred_element_type=F32)
            part = part + jnp.dot(low, stack[col, 0:TILE, :], preferred_element_type=F32)
            acc[pl.ds(row, TILE), :] += part

    s = pos_ref[0]
    for a in range(32):
        b_high = (a // HALF + s) % 2
        rows = pl.ds(a * HALF, HALF)
        keep_ref[rows, :] = acc[pl.ds(pl.multiple_of(a * 32 + b_high * HALF, HALF), HALF), :]
        send_ref[rows, :] = acc[pl.ds(pl.multiple_of(a * 32 + (1 - b_high) * HALF, HALF), HALF), :]


def split_kernel(pos_ref, keep_ref, recv_ref, direct_ref, own_ref, p1_ref, p2_ref, p3_ref, xbuf, pieces):
    n = lax.broadcasted_iota(jnp.int32, (256, 256), 0)
    g = lax.broadcasted_iota(jnp.int32, (256, 256), 1)
    base = 8 * (g // 64)
    mid = (g // 8) % 8
    low = g % 8
    place = (n == mid * 32 + base + low).astype(F32).astype(BF16)
    turned = (n == low * 32 + base + mid).astype(F32).astype(BF16)
    total = keep_ref[...] + recv_ref[...]
    direct_ref[...] = permute_lanes(total, place)
    mirrored = permute_lanes(total, turned)
    for t in range(2):
        xbuf[t] = mirrored[:, t * 128 : t * 128 + 128]
    s, x = pos_ref[0], pos_ref[1]
    left = lax.broadcasted_iota(jnp.int32, (HALF, 128), 1) < 64
    for a in range(HALF):
        rows = pl.ds(a * HALF, HALF)
        for t in range(2):
            one = xbuf[t, pl.ds(s * 256 + a, HALF, stride=HALF), :]
            two = xbuf[t, pl.ds((1 - s) * 256 + a, HALF, stride=HALF), :]
            pieces[2 * t, rows, :] = jnp.where(left, one, pltpu.roll(two, 64, 1))
            pieces[2 * t + 1, rows, :] = jnp.where(left, pltpu.roll(one, 64, 1), two)
    for k, ref in enumerate((own_ref, p1_ref, p2_ref, p3_ref)):
        ref[...] = pieces[lax.rem(x + k, NX)]


def mirror_kernel(pos_ref, direct_ref, own_ref, q1_ref, q2_ref, q3_ref, o0_ref, o1_ref, o2_ref, o3_ref, pieces, total):
    x, y = pos_ref[1], pos_ref[2]
    for k, ref in enumerate((own_ref, q1_ref, q2_ref, q3_ref)):
        pieces[lax.rem(x + NX - k, NX)] = ref[...]
    left = lax.broadcasted_iota(jnp.int32, (256, 128), 1) < 64
    for t in range(2):
        even, odd = pieces[2 * t], pieces[2 * t + 1]
        lanes = pl.ds(t * 128, 128)
        total[0:256, lanes] = direct_ref[0:256, lanes] + jnp.where(left, even, pltpu.roll(odd, 64, 1))
        total[256:512, lanes] = direct_ref[256:512, lanes] + jnp.where(left, pltpu.roll(even, 64, 1), odd)
    for k, ref in enumerate((o0_ref, o1_ref, o2_ref, o3_ref)):
        ref[...] = total[pl.ds(pl.multiple_of(lax.rem(y + k, NY) * 128, 128), 128), :]


def finish_kernel(parts_ref, denom_ref, out_ref):
    n = lax.broadcasted_iota(jnp.int32, (256, 256), 1)
    g = lax.broadcasted_iota(jnp.int32, (256, 256), 0)
    back = (n == ((g // 8) % 8) * 32 + 8 * (g // 64) + g % 8).astype(F32).astype(BF16)
    total = parts_ref[0]
    for z in range(1, NZ):
        total = total + parts_ref[z]
    out_ref[...] = permute_lanes(total, back) / denom_ref[...]


def params(mib):
    return pltpu.CompilerParams(vmem_limit_bytes=mib << 20)


def f32(*shape):
    return jax.ShapeDtypeStruct(shape, F32)


def shift_y(k):
    pairs = []
    for y in range(NY):
        to = (y + k) % NY
        for z in range(NZ):
            for core in range(2):
                core_to = core ^ (y >= 2) ^ (to >= 2)
                pairs.append(((y * NZ + z) * 2 + core, (to * NZ + z) * 2 + core_to))
    return pairs


def shift_x(k):
    return [(x, (x + k) % NX) for x in range(NX)]


def per_device(tiles, tile_slot, amplitudes, occ_energy, vir_energy):
    y, z, core, x = (lax.axis_index(name) for name in ("y", "z", "core", "occ"))
    s = lax.bitwise_xor(core, (y >= 2).astype(core.dtype))
    pos = jnp.stack([s, x, y]).astype(jnp.int32)
    smem = pl.BlockSpec(memory_space=pltpu.SMEM)
    keep, send = pl.pallas_call(
        ladder_kernel,
        in_specs=[smem, smem] + [pl.BlockSpec(memory_space=pltpu.HBM)] * 2,
        out_specs=[vmem_spec()] * 2,
        out_shape=[f32(512, 256)] * 2,
        scratch_shapes=[
            pltpu.VMEM((CAP, TILE, TILE), F32),
            pltpu.VMEM((COLS * TILE, 256), F32),
            pltpu.VMEM((COLS, 2 * TILE, 256), BF16),
            pltpu.VMEM((1024 + TILE, 256), F32),
            pltpu.SemaphoreType.DMA((CHUNKS,)),
            pltpu.SemaphoreType.DMA((CHUNKS,)),
        ],
        compiler_params=params(24),
        name="ladder",
    )(tile_slot, pos, tiles, amplitudes)
    recv = lax.ppermute(send, "core", [(0, 1), (1, 0)])
    direct, *pieces = pl.pallas_call(
        split_kernel,
        in_specs=[smem] + [vmem_spec()] * 2,
        out_specs=[vmem_spec()] * 5,
        out_shape=[f32(512, 256)] + [f32(256, 128)] * 4,
        scratch_shapes=[pltpu.VMEM((2, 512, 128), F32), pltpu.VMEM((4, 256, 128), F32)],
        compiler_params=params(16),
        name="split",
    )(pos, keep, recv)
    moved = [lax.ppermute(pieces[k], "occ", shift_x(k)) for k in range(1, NX)]
    own, *others = pl.pallas_call(
        mirror_kernel,
        in_specs=[smem] + [vmem_spec()] * 5,
        out_specs=[vmem_spec()] * 4,
        out_shape=[f32(128, 256)] * 4,
        scratch_shapes=[pltpu.VMEM((4, 256, 128), F32), pltpu.VMEM((512, 256), F32)],
        compiler_params=params(16),
        name="mirror",
    )(pos, direct, pieces[0], *moved)
    for k in range(1, NY):
        own = own + lax.ppermute(others[k - 1], VIR, shift_y(k))
    parts = lax.all_to_all(own.reshape(NZ, HALF, 256), "z", 0, 0)

    def pick(table, index):
        orbital = lax.broadcasted_iota(jnp.int32, (index.shape[0], 32), 1)
        return jnp.sum(jnp.where(index[:, None] == orbital, table[None, :], 0.0), axis=1)

    n = lax.broadcasted_iota(jnp.int32, (256,), 0)
    row = lax.broadcasted_iota(jnp.int32, (HALF,), 0)
    pair = pick(occ_energy, x * 8 + n // 32) + pick(occ_energy, n % 32)
    first = pick(vir_energy, jnp.full((HALF,), y * NZ + z, jnp.int32))
    second = pick(vir_energy, core * HALF + row)
    denominator = pair[None, :] - first[:, None] - second[:, None]
    return pl.pallas_call(
        finish_kernel,
        in_specs=[vmem_spec()] * 2,
        out_specs=vmem_spec(),
        out_shape=f32(HALF, 256),
        compiler_params=params(16),
        name="finish",
    )(parts, denominator)


def solution(mesh):
    fine = Mesh(mesh.devices.reshape(NY, NZ, 2, NX), ("y", "z", "core", "occ"))
    in_specs = (P(VIR, None, None), P(VIR), P(VIR, "occ"), P(), P())
    return jax.shard_map(
        per_device, mesh=fine, in_specs=in_specs, out_specs=P(VIR, "occ"), check_vma=False
    )
```

```python
import functools

import jax
import jax.numpy as jnp
from jax import lax
from jax.experimental import pallas as pl
from jax.experimental.pallas import tpu as pltpu
from jax.sharding import Mesh
from jax.sharding import PartitionSpec as P

F32 = jnp.float32
BF16 = jnp.bfloat16
TILE = 128
CAP = 64
COLS = 32
CHUNKS = 8
NY, NZ, NX = 4, 8, 4
HALF = 16
EIGHT = 8
VIR = ("y", "z", "core")


def vmem_spec():
    return pl.BlockSpec(memory_space=pltpu.VMEM)


def split3(x):
    top = x.astype(BF16)
    rest = x - top.astype(F32)
    mid = rest.astype(BF16)
    low = (rest - mid.astype(F32)).astype(BF16)
    return top, mid, low


def permute_lanes(x, place):
    top, mid, low = split3(x)
    out = jnp.dot(low, place, preferred_element_type=F32)
    out = out + jnp.dot(mid, place, preferred_element_type=F32)
    return out + jnp.dot(top, place, preferred_element_type=F32)


def row_set(y, core):
    return lax.bitwise_xor(core, (y >= NY // 2).astype(jnp.int32))


def place(name):
    return lax.axis_index(name).astype(jnp.int32)


def ladder_kernel(slot_hbm, tiles_hbm, amps_hbm, *rest):
    outs, (slots, tbuf, abuf, stack, acc, ssem, tsem, asem) = rest[:2], rest[2:]
    arows, trows = abuf.shape[0] // CHUNKS, CAP // CHUNKS

    def amp_copy(c):
        rows = pl.ds(c * arows, arows)
        return pltpu.make_async_copy(amps_hbm.at[rows], abuf.at[rows], asem.at[c])

    def tile_copy(c):
        rows = pl.ds(c * trows, trows)
        return pltpu.make_async_copy(tiles_hbm.at[rows], tbuf.at[rows], tsem.at[c])

    slot_copy = pltpu.make_async_copy(slot_hbm, slots, ssem)
    slot_copy.start()
    for c in range(CHUNKS):
        amp_copy(c).start()
    for c in range(CHUNKS):
        tile_copy(c).start()
    acc[...] = jnp.zeros_like(acc)

    @pl.loop(0, CHUNKS)
    def _(c):
        amp_copy(c).wait()
        for q in range(arows // TILE):
            block = c * (arows // TILE) + q
            a = abuf[pl.ds(pl.multiple_of(block * TILE, TILE), TILE), :]
            top = a.astype(BF16)
            stack[block, 0:TILE, :] = top
            stack[block, TILE : 2 * TILE, :] = (a - top.astype(F32)).astype(BF16)

    slot_copy.wait()

    @pl.loop(0, CHUNKS)
    def _(c):
        tile_copy(c).wait()
        for u in range(trows):
            slot = slots[c * trows + u]
            row = pl.multiple_of((slot // COLS) * TILE, TILE)
            col = slot % COLS
            t = tbuf[c * trows + u]
            top = t.astype(BF16)
            low = (t - top.astype(F32)).astype(BF16)
            part = jnp.dot(jnp.concatenate([top, top], axis=1), stack[col], preferred_element_type=F32)
            part = part + jnp.dot(low, stack[col, 0:TILE, :], preferred_element_type=F32)
            acc[pl.ds(row, TILE), :] += part

    s = row_set(place("y"), place("core"))
    for a in range(32):
        for own in range(2):
            b_high = (a // HALF + s + own) % 2
            row = pl.multiple_of(a * 32 + b_high * HALF, HALF)
            outs[own][pl.ds(a * HALF, HALF), :] = acc[pl.ds(row, HALF), :]


def column_order(turned):
    n = lax.broadcasted_iota(jnp.int32, (256, 256), 0)
    g = lax.broadcasted_iota(jnp.int32, (256, 256), 1)
    outer, inner = (g // EIGHT) % EIGHT, g % EIGHT
    if turned:
        outer, inner = inner, outer
    return (n == outer * 32 + EIGHT * (g // 64) + inner).astype(F32).astype(BF16)


def split_kernel(keep_ref, recv_ref, own_ref, p1_ref, p2_ref, p3_ref, xbuf, pieces):
    mirrored = permute_lanes(keep_ref[...] + recv_ref[...], column_order(True))
    for t in range(2):
        xbuf[t] = mirrored[:, t * 128 : t * 128 + 128]
    s, x = row_set(place("y"), place("core")), place("occ")
    left = lax.broadcasted_iota(jnp.int32, (HALF, 128), 1) < 64
    for a in range(HALF):
        rows = pl.ds(a * HALF, HALF)
        for t in range(2):
            one = xbuf[t, pl.ds(s * 256 + a, HALF, stride=HALF), :]
            two = xbuf[t, pl.ds((1 - s) * 256 + a, HALF, stride=HALF), :]
            pieces[2 * t, rows, :] = jnp.where(left, one, pltpu.roll(two, 64, 1))
            pieces[2 * t + 1, rows, :] = jnp.where(left, pltpu.roll(one, 64, 1), two)
    for k, ref in enumerate((own_ref, p1_ref, p2_ref, p3_ref)):
        ref[...] = pieces[lax.rem(x + k, NX)]


def direct_kernel(keep_ref, recv_ref, out_ref):
    out_ref[...] = permute_lanes(keep_ref[...] + recv_ref[...], column_order(False))


def mirror_kernel(direct_ref, own_ref, q1_ref, q2_ref, q3_ref, o0_ref, o1_ref, o2_ref, o3_ref, pieces, total):
    x, y = place("occ"), place("y")
    for k, ref in enumerate((own_ref, q1_ref, q2_ref, q3_ref)):
        pieces[lax.rem(x + NX - k, NX)] = ref[...]
    left = lax.broadcasted_iota(jnp.int32, (256, 128), 1) < 64
    for t in range(2):
        even, odd = pieces[2 * t], pieces[2 * t + 1]
        lanes = pl.ds(t * 128, 128)
        total[0:256, lanes] = direct_ref[0:256, lanes] + jnp.where(left, even, pltpu.roll(odd, 64, 1))
        total[256:512, lanes] = direct_ref[256:512, lanes] + jnp.where(left, pltpu.roll(even, 64, 1), odd)
    for k, ref in enumerate((o0_ref, o1_ref, o2_ref, o3_ref)):
        ref[...] = total[pl.ds(pl.multiple_of(lax.rem(y + k, NY) * 128, 128), 128), :]


def finish_kernel(parts_ref, denom_ref, out_ref):
    n = lax.broadcasted_iota(jnp.int32, (256, 256), 1)
    g = lax.broadcasted_iota(jnp.int32, (256, 256), 0)
    back = (n == ((g // 8) % 8) * 32 + 8 * (g // 64) + g % 8).astype(F32).astype(BF16)
    acc = parts_ref[0]
    for z in range(1, NZ):
        acc = acc + parts_ref[z]
    out_ref[...] = permute_lanes(acc, back) / denom_ref[...]


def params(mib):
    return pltpu.CompilerParams(vmem_limit_bytes=mib << 20)


def f32(*shape):
    return jax.ShapeDtypeStruct(shape, F32)


def kernel_call(body, name, args, outs, scratch=()):
    single = not isinstance(outs, list)
    return pl.pallas_call(
        body,
        in_specs=[vmem_spec()] * len(args),
        out_specs=vmem_spec() if single else [vmem_spec()] * len(outs),
        out_shape=outs,
        scratch_shapes=[pltpu.VMEM(shape, F32) for shape in scratch],
        compiler_params=params(8),
        name=name,
    )(*args)


def shift_y(k):
    pairs = []
    for y in range(NY):
        to = (y + k) % NY
        for z in range(NZ):
            for core in range(2):
                core_to = core ^ (y >= 2) ^ (to >= 2)
                pairs.append(((y * NZ + z) * 2 + core, (to * NZ + z) * 2 + core_to))
    return pairs


def shift_x(k):
    return [(x, (x + k) % NX) for x in range(NX)]


def in_hbm(x):
    return pltpu.with_memory_space_constraint(x, pltpu.HBM)


def per_device(tiles, tile_slot, amplitudes, occ_energy, vir_energy):
    y, z, core, x = (place(name) for name in ("y", "z", "core", "occ"))
    keep, send = pl.pallas_call(
        ladder_kernel,
        in_specs=[pl.BlockSpec(memory_space=pltpu.HBM)] * 3,
        out_specs=[vmem_spec()] * 2,
        out_shape=[f32(512, 256)] * 2,
        scratch_shapes=[
            pltpu.SMEM((CAP,), jnp.int32),
            pltpu.VMEM((CAP, TILE, TILE), F32),
            pltpu.VMEM((COLS * TILE, 256), F32),
            pltpu.VMEM((COLS, 2 * TILE, 256), BF16),
            pltpu.VMEM((1024 + TILE, 256), F32),
            pltpu.SemaphoreType.DMA,
            pltpu.SemaphoreType.DMA((CHUNKS,)),
            pltpu.SemaphoreType.DMA((CHUNKS,)),
        ],
        compiler_params=params(24),
        name="ladder",
    )(in_hbm(tile_slot), in_hbm(tiles), in_hbm(amplitudes))
    recv = lax.ppermute(send, "core", [(0, 1), (1, 0)])
    pieces = kernel_call(
        split_kernel, "split", [keep, recv], [f32(256, 128)] * 4, [(2, 512, 128), (4, 256, 128)]
    )
    moved = [lax.ppermute(pieces[k], "occ", shift_x(k)) for k in range(1, NX)]
    direct = kernel_call(direct_kernel, "direct", [keep, recv], f32(512, 256))
    own, *others = kernel_call(
        mirror_kernel, "mirror", [direct, pieces[0], *moved], [f32(128, 256)] * 4, [(4, 256, 128), (512, 256)]
    )
    for k in range(1, NY):
        own = own + lax.ppermute(others[k - 1], VIR, shift_y(k))
    parts = lax.all_to_all(own.reshape(NZ, HALF, 256), "z", 0, 0)

    def pick(table, index):
        orbital = lax.broadcasted_iota(jnp.int32, (index.shape[0], 32), 1)
        return jnp.sum(jnp.where(index[:, None] == orbital, table[None, :], 0.0), axis=1)

    n = lax.broadcasted_iota(jnp.int32, (256,), 0)
    row = lax.broadcasted_iota(jnp.int32, (HALF,), 0)
    pair = pick(occ_energy, x * 8 + n // 32) + pick(occ_energy, n % 32)
    first = pick(vir_energy, jnp.full((HALF,), y * NZ + z, jnp.int32))
    second = pick(vir_energy, core * HALF + row)
    denominator = pair[None, :] - first[:, None] - second[:, None]
    return kernel_call(finish_kernel, "finish", [parts, denominator], f32(HALF, 256))


def solution(mesh):
    fine = Mesh(mesh.devices.reshape(NY, NZ, 2, NX), ("y", "z", "core", "occ"))
    in_specs = (P(VIR, None, None), P(VIR), P(VIR, "occ"), P(), P())
    return jax.shard_map(
        per_device, mesh=fine, in_specs=in_specs, out_specs=P(VIR, "occ"), check_vma=False
    )
```

```python
import functools

import jax
import jax.numpy as jnp
from jax import lax
from jax.experimental import pallas as pl
from jax.experimental.pallas import tpu as pltpu
from jax.sharding import Mesh
from jax.sharding import PartitionSpec as P

F32 = jnp.float32
BF16 = jnp.bfloat16
TILE = 128
CAP = 64
COLS = 32
CHUNKS = 8
NY, NZ, NX = 4, 8, 4
HALF = 16
EIGHT = 8
VIR = ("y", "z", "core")
Z_ORDER = (4, 5, 6, 7, 0, 1, 2, 3)


def vmem_spec():
    return pl.BlockSpec(memory_space=pltpu.VMEM)


def split3(x):
    top = x.astype(BF16)
    rest = x - top.astype(F32)
    mid = rest.astype(BF16)
    low = (rest - mid.astype(F32)).astype(BF16)
    return top, mid, low


def permute_lanes(x, place):
    top, mid, low = split3(x)
    out = jnp.dot(low, place, preferred_element_type=F32)
    out = out + jnp.dot(mid, place, preferred_element_type=F32)
    return out + jnp.dot(top, place, preferred_element_type=F32)


def row_set(y, core):
    return lax.bitwise_xor(core, (y >= NY // 2).astype(jnp.int32))


def place(name):
    return lax.axis_index(name).astype(jnp.int32)


def turn(position, k, size, which):
    return lax.rem(position + size + k * (1 - 2 * which), size)


def ladder_kernel(slot_hbm, tiles_hbm, amps_hbm, *rest):
    outs, (slots, tbuf, abuf, stack, acc, ssem, tsem, asem) = rest[:2], rest[2:]
    arows, trows = abuf.shape[0] // CHUNKS, CAP // CHUNKS

    def amp_copy(c):
        rows = pl.ds(c * arows, arows)
        return pltpu.make_async_copy(amps_hbm.at[rows], abuf.at[rows], asem.at[c])

    def tile_copy(c):
        rows = pl.ds(c * trows, trows)
        return pltpu.make_async_copy(tiles_hbm.at[rows], tbuf.at[rows], tsem.at[c])

    slot_copy = pltpu.make_async_copy(slot_hbm, slots, ssem)
    slot_copy.start()
    for c in range(CHUNKS):
        amp_copy(c).start()
    for c in range(CHUNKS):
        tile_copy(c).start()
    acc[...] = jnp.zeros_like(acc)

    @pl.loop(0, CHUNKS)
    def _(c):
        amp_copy(c).wait()
        for q in range(arows // TILE):
            block = c * (arows // TILE) + q
            a = abuf[pl.ds(pl.multiple_of(block * TILE, TILE), TILE), :]
            top = a.astype(BF16)
            stack[block, 0:TILE, :] = top
            stack[block, TILE : 2 * TILE, :] = (a - top.astype(F32)).astype(BF16)

    slot_copy.wait()

    @pl.loop(0, CHUNKS)
    def _(c):
        tile_copy(c).wait()
        for u in range(trows):
            slot = slots[c * trows + u]
            row = pl.multiple_of((slot // COLS) * TILE, TILE)
            col = slot % COLS
            t = tbuf[c * trows + u]
            top = t.astype(BF16)
            low = (t - top.astype(F32)).astype(BF16)
            part = jnp.dot(jnp.concatenate([top, top], axis=1), stack[col], preferred_element_type=F32)
            part = part + jnp.dot(low, stack[col, 0:TILE, :], preferred_element_type=F32)
            acc[pl.ds(row, TILE), :] += part

    s = row_set(place("y"), place("core"))
    for a in range(32):
        for own in range(2):
            b_high = (a // HALF + s + own) % 2
            row = pl.multiple_of(a * 32 + b_high * HALF, HALF)
            outs[own][pl.ds(a * HALF, HALF), :] = acc[pl.ds(row, HALF), :]


def column_order(turned):
    n = lax.broadcasted_iota(jnp.int32, (256, 256), 0)
    g = lax.broadcasted_iota(jnp.int32, (256, 256), 1)
    outer, inner = (g // EIGHT) % EIGHT, g % EIGHT
    if turned:
        outer, inner = inner, outer
    return (n == outer * 32 + EIGHT * (g // 64) + inner).astype(F32).astype(BF16)


def split_kernel(keep_ref, recv_ref, own_ref, p1_ref, p2_ref, p3_ref, xbuf, pieces):
    mirrored = permute_lanes(keep_ref[...] + recv_ref[...], column_order(True))
    for t in range(2):
        xbuf[t] = mirrored[:, t * 128 : t * 128 + 128]
    s, x = row_set(place("y"), place("core")), place("occ")
    left = lax.broadcasted_iota(jnp.int32, (HALF, 128), 1) < 64
    for a in range(HALF):
        rows = pl.ds(a * HALF, HALF)
        for t in range(2):
            one = xbuf[t, pl.ds(s * 256 + a, HALF, stride=HALF), :]
            two = xbuf[t, pl.ds((1 - s) * 256 + a, HALF, stride=HALF), :]
            pieces[2 * t, rows, :] = jnp.where(left, one, pltpu.roll(two, 64, 1))
            pieces[2 * t + 1, rows, :] = jnp.where(left, pltpu.roll(one, 64, 1), two)
    for k, ref in enumerate((own_ref, p1_ref, p2_ref, p3_ref)):
        ref[...] = pieces[turn(x, k, NX, place("core"))]


def direct_kernel(keep_ref, recv_ref, out_ref):
    out_ref[...] = permute_lanes(keep_ref[...] + recv_ref[...], column_order(False))


def mirror_kernel(direct_ref, own_ref, q1_ref, q2_ref, q3_ref, o0_ref, o1_ref, o2_ref, o3_ref, pieces, total):
    x, y, core = place("occ"), place("y"), place("core")
    for k, ref in enumerate((own_ref, q1_ref, q2_ref, q3_ref)):
        pieces[turn(x, -k, NX, core)] = ref[...]
    left = lax.broadcasted_iota(jnp.int32, (256, 128), 1) < 64
    for t in range(2):
        even, odd = pieces[2 * t], pieces[2 * t + 1]
        lanes = pl.ds(t * 128, 128)
        total[0:256, lanes] = direct_ref[0:256, lanes] + jnp.where(left, even, pltpu.roll(odd, 64, 1))
        total[256:512, lanes] = direct_ref[256:512, lanes] + jnp.where(left, pltpu.roll(even, 64, 1), odd)
    for k, ref in enumerate((o0_ref, o1_ref, o2_ref, o3_ref)):
        ref[...] = total[pl.ds(pl.multiple_of(turn(y, k, NY, row_set(y, core)) * 128, 128), 128), :]


def gather_kernel(r0_ref, r1_ref, r2_ref, r3_ref, out_ref):
    for p, z in enumerate(Z_ORDER):
        rows = pl.ds(z * HALF, HALF)
        out_ref[p] = (r0_ref[rows, :] + r1_ref[rows, :]) + (r2_ref[rows, :] + r3_ref[rows, :])


def finish_kernel(parts_ref, denom_ref, out_ref):
    n = lax.broadcasted_iota(jnp.int32, (256, 256), 1)
    g = lax.broadcasted_iota(jnp.int32, (256, 256), 0)
    back = (n == ((g // 8) % 8) * 32 + 8 * (g // 64) + g % 8).astype(F32).astype(BF16)
    acc = parts_ref[0]
    for z in range(1, NZ):
        acc = acc + parts_ref[z]
    out_ref[...] = permute_lanes(acc, back) / denom_ref[...]


def params(mib):
    return pltpu.CompilerParams(vmem_limit_bytes=mib << 20)


def f32(*shape):
    return jax.ShapeDtypeStruct(shape, F32)


def kernel_call(body, name, args, outs, scratch=()):
    single = not isinstance(outs, list)
    return pl.pallas_call(
        body,
        in_specs=[vmem_spec()] * len(args),
        out_specs=vmem_spec() if single else [vmem_spec()] * len(outs),
        out_shape=outs,
        scratch_shapes=[pltpu.VMEM(shape, F32) for shape in scratch],
        compiler_params=params(8),
        name=name,
    )(*args)


def shift_y(k):
    pairs = []
    for y in range(NY):
        for z in range(NZ):
            for core in range(2):
                s = core ^ (y >= NY // 2)
                to = (y + (k if s == 0 else -k)) % NY
                core_to = s ^ (to >= NY // 2)
                pairs.append(((y * NZ + z) * 2 + core, (to * NZ + z) * 2 + core_to))
    return pairs


def shift_x(k):
    return [
        (core * NX + x, core * NX + (x + (k if core == 0 else -k)) % NX) for core in range(2) for x in range(NX)
    ]


def z_groups():
    return [[(y * NZ + z) * 2 + core for z in Z_ORDER] for y in range(NY) for core in range(2)]


def in_hbm(x):
    return pltpu.with_memory_space_constraint(x, pltpu.HBM)


def per_device(tiles, tile_slot, amplitudes, occ_energy, vir_energy):
    y, z, core, x = (place(name) for name in ("y", "z", "core", "occ"))
    keep, send = pl.pallas_call(
        ladder_kernel,
        in_specs=[pl.BlockSpec(memory_space=pltpu.HBM)] * 3,
        out_specs=[vmem_spec()] * 2,
        out_shape=[f32(512, 256)] * 2,
        scratch_shapes=[
            pltpu.SMEM((CAP,), jnp.int32),
            pltpu.VMEM((CAP, TILE, TILE), F32),
            pltpu.VMEM((COLS * TILE, 256), F32),
            pltpu.VMEM((COLS, 2 * TILE, 256), BF16),
            pltpu.VMEM((1024 + TILE, 256), F32),
            pltpu.SemaphoreType.DMA,
            pltpu.SemaphoreType.DMA((CHUNKS,)),
            pltpu.SemaphoreType.DMA((CHUNKS,)),
        ],
        compiler_params=params(24),
        name="ladder",
    )(in_hbm(tile_slot), in_hbm(tiles), in_hbm(amplitudes))
    recv = lax.ppermute(send, "core", [(0, 1), (1, 0)])
    pieces = kernel_call(
        split_kernel, "split", [keep, recv], [f32(256, 128)] * 4, [(2, 512, 128), (4, 256, 128)]
    )
    moved = [lax.ppermute(pieces[k], ("core", "occ"), shift_x(k)) for k in range(1, NX)]
    direct = kernel_call(direct_kernel, "direct", [keep, recv], f32(512, 256))
    own, *others = kernel_call(
        mirror_kernel, "mirror", [direct, pieces[0], *moved], [f32(128, 256)] * 4, [(4, 256, 128), (512, 256)]
    )
    moved = [lax.ppermute(others[k - 1], VIR, shift_y(k)) for k in range(1, NY)]
    summed = kernel_call(gather_kernel, "gather", [own, *moved], f32(NZ, HALF, 256))
    parts = lax.all_to_all(summed, VIR, 0, 0, axis_index_groups=z_groups())

    def pick(table, index):
        orbital = lax.broadcasted_iota(jnp.int32, (index.shape[0], 32), 1)
        return jnp.sum(jnp.where(index[:, None] == orbital, table[None, :], 0.0), axis=1)

    n = lax.broadcasted_iota(jnp.int32, (256,), 0)
    row = lax.broadcasted_iota(jnp.int32, (HALF,), 0)
    pair = pick(occ_energy, x * 8 + n // 32) + pick(occ_energy, n % 32)
    first = pick(vir_energy, jnp.full((HALF,), y * NZ + z, jnp.int32))
    second = pick(vir_energy, core * HALF + row)
    denominator = pair[None, :] - first[:, None] - second[:, None]
    return kernel_call(finish_kernel, "finish", [parts, denominator], f32(HALF, 256))


def solution(mesh):
    fine = Mesh(mesh.devices.reshape(NY, NZ, 2, NX), ("y", "z", "core", "occ"))
    in_specs = (P(VIR, None, None), P(VIR), P(VIR, "occ"), P(), P())
    return jax.shard_map(
        per_device, mesh=fine, in_specs=in_specs, out_specs=P(VIR, "occ"), check_vma=False
    )
```

```python
import functools

import jax
import jax.numpy as jnp
from jax import lax
from jax.experimental import pallas as pl
from jax.experimental.pallas import tpu as pltpu
from jax.sharding import Mesh
from jax.sharding import PartitionSpec as P

F32 = jnp.float32
BF16 = jnp.bfloat16
TILE = 128
CAP = 64
COLS = 32
CHUNKS = 4
NY, NZ, NX = 4, 8, 4
STEPS = (0, 2, 1, 3)
HALF = 16
EIGHT = 8
VIR = ("y", "z", "core")
Z_ORDER = (4, 5, 6, 7, 0, 1, 2, 3)


def vmem_spec():
    return pl.BlockSpec(memory_space=pltpu.VMEM)


def split3(x):
    top = x.astype(BF16)
    rest = x - top.astype(F32)
    mid = rest.astype(BF16)
    low = (rest - mid.astype(F32)).astype(BF16)
    return top, mid, low


def permute_lanes(x, place):
    top, mid, low = split3(x)
    out = jnp.dot(low, place, preferred_element_type=F32)
    out = out + jnp.dot(mid, place, preferred_element_type=F32)
    return out + jnp.dot(top, place, preferred_element_type=F32)


def row_set(y, core):
    return lax.bitwise_xor(core, (y >= NY // 2).astype(jnp.int32))


def place(name):
    return lax.axis_index(name).astype(jnp.int32)


def turn(position, k, size, which):
    return lax.rem(position + size + k * (1 - 2 * which), size)


def ladder_kernel(slot_hbm, tiles_hbm, amps_hbm, *rest):
    outs, (slots, tbuf, abuf, stack, acc, ssem, tsem, asem) = rest[:2], rest[2:]
    arows, trows = abuf.shape[0] // CHUNKS, CAP // CHUNKS

    def amp_copy(c):
        rows = pl.ds(c * arows, arows)
        return pltpu.make_async_copy(amps_hbm.at[rows], abuf.at[rows], asem.at[c])

    def tile_copy(c):
        rows = pl.ds(c * trows, trows)
        return pltpu.make_async_copy(tiles_hbm.at[rows], tbuf.at[rows], tsem.at[c])

    slot_copy = pltpu.make_async_copy(slot_hbm, slots, ssem)
    slot_copy.start()
    for c in range(CHUNKS):
        amp_copy(c).start()
    acc[...] = jnp.zeros_like(acc)

    @pl.loop(0, CHUNKS)
    def _(c):
        amp_copy(c).wait()
        tile_copy(c).start()
        for q in range(arows // TILE):
            block = c * (arows // TILE) + q
            a = abuf[pl.ds(pl.multiple_of(block * TILE, TILE), TILE), :]
            top = a.astype(BF16)
            stack[block, 0:TILE, :] = top
            stack[block, TILE : 2 * TILE, :] = (a - top.astype(F32)).astype(BF16)

    slot_copy.wait()

    @pl.loop(0, CHUNKS)
    def _(c):
        tile_copy(c).wait()
        for u in range(trows):
            slot = slots[c * trows + u]
            row = pl.multiple_of((slot // COLS) * TILE, TILE)
            col = slot % COLS
            t = tbuf[c * trows + u]
            top = t.astype(BF16)
            low = (t - top.astype(F32)).astype(BF16)
            part = jnp.dot(jnp.concatenate([top, top], axis=1), stack[col], preferred_element_type=F32)
            part = part + jnp.dot(low, stack[col, 0:TILE, :], preferred_element_type=F32)
            acc[pl.ds(row, TILE), :] += part

    s = row_set(place("y"), place("core"))
    for a in range(32):
        for own in range(2):
            b_high = (a // HALF + s + own) % 2
            row = pl.multiple_of(a * 32 + b_high * HALF, HALF)
            outs[own][pl.ds(a * HALF, HALF), :] = acc[pl.ds(row, HALF), :]


def column_order(turned):
    n = lax.broadcasted_iota(jnp.int32, (256, 256), 0)
    g = lax.broadcasted_iota(jnp.int32, (256, 256), 1)
    outer, inner = (g // EIGHT) % EIGHT, g % EIGHT
    if turned:
        outer, inner = inner, outer
    return (n == outer * 32 + EIGHT * (g // 64) + inner).astype(F32).astype(BF16)


def split_kernel(keep_ref, recv_ref, own_ref, p1_ref, p2_ref, p3_ref, xbuf, pieces):
    mirrored = permute_lanes(keep_ref[...] + recv_ref[...], column_order(True))
    for t in range(2):
        xbuf[t] = mirrored[:, t * 128 : t * 128 + 128]
    s, x = row_set(place("y"), place("core")), place("occ")
    left = lax.broadcasted_iota(jnp.int32, (HALF, 128), 1) < 64
    for a in range(HALF):
        rows = pl.ds(a * HALF, HALF)
        for t in range(2):
            one = xbuf[t, pl.ds(s * 256 + a, HALF, stride=HALF), :]
            two = xbuf[t, pl.ds((1 - s) * 256 + a, HALF, stride=HALF), :]
            pieces[2 * t, rows, :] = jnp.where(left, one, pltpu.roll(two, 64, 1))
            pieces[2 * t + 1, rows, :] = jnp.where(left, pltpu.roll(one, 64, 1), two)
    for k, ref in zip(STEPS, (own_ref, p1_ref, p2_ref, p3_ref)):
        ref[...] = pieces[turn(x, k, NX, place("core"))]


def direct_kernel(keep_ref, recv_ref, out_ref):
    out_ref[...] = permute_lanes(keep_ref[...] + recv_ref[...], column_order(False))


def mirror_kernel(direct_ref, own_ref, q1_ref, q2_ref, q3_ref, o0_ref, o1_ref, o2_ref, o3_ref, pieces, total):
    x, y, core = place("occ"), place("y"), place("core")
    for k, ref in zip(STEPS, (own_ref, q1_ref, q2_ref, q3_ref)):
        pieces[turn(x, -k, NX, core)] = ref[...]
    left = lax.broadcasted_iota(jnp.int32, (256, 128), 1) < 64
    for t in range(2):
        even, odd = pieces[2 * t], pieces[2 * t + 1]
        lanes = pl.ds(t * 128, 128)
        total[0:256, lanes] = direct_ref[0:256, lanes] + jnp.where(left, even, pltpu.roll(odd, 64, 1))
        total[256:512, lanes] = direct_ref[256:512, lanes] + jnp.where(left, pltpu.roll(even, 64, 1), odd)
    for k, ref in zip(STEPS, (o0_ref, o1_ref, o2_ref, o3_ref)):
        ref[...] = total[pl.ds(pl.multiple_of(turn(y, k, NY, row_set(y, core)) * 128, 128), 128), :]


def gather_kernel(r0_ref, r1_ref, r2_ref, r3_ref, out_ref):
    for p, z in enumerate(Z_ORDER):
        rows = pl.ds(z * HALF, HALF)
        out_ref[p] = (r0_ref[rows, :] + r1_ref[rows, :]) + (r2_ref[rows, :] + r3_ref[rows, :])


def finish_kernel(parts_ref, denom_ref, out_ref):
    n = lax.broadcasted_iota(jnp.int32, (256, 256), 1)
    g = lax.broadcasted_iota(jnp.int32, (256, 256), 0)
    back = (n == ((g // 8) % 8) * 32 + 8 * (g // 64) + g % 8).astype(F32).astype(BF16)
    acc = parts_ref[0]
    for z in range(1, NZ):
        acc = acc + parts_ref[z]
    out_ref[...] = permute_lanes(acc, back) / denom_ref[...]


def params(mib):
    return pltpu.CompilerParams(vmem_limit_bytes=mib << 20)


def f32(*shape):
    return jax.ShapeDtypeStruct(shape, F32)


def kernel_call(body, name, args, outs, scratch=()):
    single = not isinstance(outs, list)
    return pl.pallas_call(
        body,
        in_specs=[vmem_spec()] * len(args),
        out_specs=vmem_spec() if single else [vmem_spec()] * len(outs),
        out_shape=outs,
        scratch_shapes=[pltpu.VMEM(shape, F32) for shape in scratch],
        compiler_params=params(8),
        name=name,
    )(*args)


def shift_y(k):
    pairs = []
    for y in range(NY):
        for z in range(NZ):
            for core in range(2):
                s = core ^ (y >= NY // 2)
                to = (y + (k if s == 0 else -k)) % NY
                core_to = s ^ (to >= NY // 2)
                pairs.append(((y * NZ + z) * 2 + core, (to * NZ + z) * 2 + core_to))
    return pairs


def shift_x(k):
    return [
        (core * NX + x, core * NX + (x + (k if core == 0 else -k)) % NX) for core in range(2) for x in range(NX)
    ]


def z_groups():
    return [[(y * NZ + z) * 2 + core for z in Z_ORDER] for y in range(NY) for core in range(2)]


def in_hbm(x):
    return pltpu.with_memory_space_constraint(x, pltpu.HBM)


def per_device(tiles, tile_slot, amplitudes, occ_energy, vir_energy):
    y, z, core, x = (place(name) for name in ("y", "z", "core", "occ"))
    keep, send = pl.pallas_call(
        ladder_kernel,
        in_specs=[pl.BlockSpec(memory_space=pltpu.HBM)] * 3,
        out_specs=[vmem_spec()] * 2,
        out_shape=[f32(512, 256)] * 2,
        scratch_shapes=[
            pltpu.SMEM((CAP,), jnp.int32),
            pltpu.VMEM((CAP, TILE, TILE), F32),
            pltpu.VMEM((COLS * TILE, 256), F32),
            pltpu.VMEM((COLS, 2 * TILE, 256), BF16),
            pltpu.VMEM((1024 + TILE, 256), F32),
            pltpu.SemaphoreType.DMA,
            pltpu.SemaphoreType.DMA((CHUNKS,)),
            pltpu.SemaphoreType.DMA((CHUNKS,)),
        ],
        compiler_params=params(24),
        name="ladder",
    )(in_hbm(tile_slot), in_hbm(tiles), in_hbm(amplitudes))
    recv = lax.ppermute(send, "core", [(0, 1), (1, 0)])
    pieces = kernel_call(
        split_kernel, "split", [keep, recv], [f32(256, 128)] * 4, [(2, 512, 128), (4, 256, 128)]
    )
    moved = [lax.ppermute(pieces[n], ("core", "occ"), shift_x(STEPS[n])) for n in range(1, NX)]
    direct = kernel_call(direct_kernel, "direct", [keep, recv], f32(512, 256))
    own, *others = kernel_call(
        mirror_kernel, "mirror", [direct, pieces[0], *moved], [f32(128, 256)] * 4, [(4, 256, 128), (512, 256)]
    )
    moved = [lax.ppermute(others[n - 1], VIR, shift_y(STEPS[n])) for n in range(1, NY)]
    summed = kernel_call(gather_kernel, "gather", [own, *moved], f32(NZ, HALF, 256))
    parts = lax.all_to_all(summed, VIR, 0, 0, axis_index_groups=z_groups())

    def pick(table, index):
        orbital = lax.broadcasted_iota(jnp.int32, (index.shape[0], 32), 1)
        return jnp.sum(jnp.where(index[:, None] == orbital, table[None, :], 0.0), axis=1)

    n = lax.broadcasted_iota(jnp.int32, (256,), 0)
    row = lax.broadcasted_iota(jnp.int32, (HALF,), 0)
    pair = pick(occ_energy, x * 8 + n // 32) + pick(occ_energy, n % 32)
    first = pick(vir_energy, jnp.full((HALF,), y * NZ + z, jnp.int32))
    second = pick(vir_energy, core * HALF + row)
    denominator = pair[None, :] - first[:, None] - second[:, None]
    return kernel_call(finish_kernel, "finish", [parts, denominator], f32(HALF, 256))


def solution(mesh):
    fine = Mesh(mesh.devices.reshape(NY, NZ, 2, NX), ("y", "z", "core", "occ"))
    in_specs = (P(VIR, None, None), P(VIR), P(VIR, "occ"), P(), P())
    return jax.shard_map(
        per_device, mesh=fine, in_specs=in_specs, out_specs=P(VIR, "occ"), check_vma=False
    )
```

```python
import functools

import jax
import jax.numpy as jnp
from jax import lax
from jax.experimental import pallas as pl
from jax.experimental.pallas import tpu as pltpu
from jax.sharding import Mesh
from jax.sharding import PartitionSpec as P

F32 = jnp.float32
BF16 = jnp.bfloat16
TILE = 128
CAP = 64
COLS = 32
CHUNKS = 4
NY, NZ, NX = 4, 8, 4
STEPS = (0, 2, 1, 3)
YSTEPS = (0, 2, 3, 1)
HALF = 16
EIGHT = 8
VIR = ("y", "z", "core")
Z_ORDER = (4, 5, 6, 7, 0, 1, 2, 3)


def vmem_spec():
    return pl.BlockSpec(memory_space=pltpu.VMEM)


def split3(x):
    top = x.astype(BF16)
    rest = x - top.astype(F32)
    mid = rest.astype(BF16)
    low = (rest - mid.astype(F32)).astype(BF16)
    return top, mid, low


def permute_lanes(x, place):
    top, mid, low = split3(x)
    out = jnp.dot(low, place, preferred_element_type=F32)
    out = out + jnp.dot(mid, place, preferred_element_type=F32)
    return out + jnp.dot(top, place, preferred_element_type=F32)


def row_set(y, core):
    return lax.bitwise_xor(core, (y >= NY // 2).astype(jnp.int32))


def place(name):
    return lax.axis_index(name).astype(jnp.int32)


def turn(position, k, size, which):
    return lax.rem(position + size + k * (1 - 2 * which), size)


def ladder_kernel(slot_hbm, tiles_hbm, amps_hbm, *rest):
    outs, (slots, tbuf, abuf, stack, acc, ssem, tsem, asem) = rest[:2], rest[2:]
    arows, trows = abuf.shape[0] // CHUNKS, CAP // CHUNKS

    def amp_copy(c):
        rows = pl.ds(c * arows, arows)
        return pltpu.make_async_copy(amps_hbm.at[rows], abuf.at[rows], asem.at[c])

    def tile_copy(c):
        rows = pl.ds(c * trows, trows)
        return pltpu.make_async_copy(tiles_hbm.at[rows], tbuf.at[rows], tsem.at[c])

    slot_copy = pltpu.make_async_copy(slot_hbm, slots, ssem)
    slot_copy.start()
    for c in range(CHUNKS):
        amp_copy(c).start()
    acc[...] = jnp.zeros_like(acc)

    @pl.loop(0, CHUNKS)
    def _(c):
        amp_copy(c).wait()
        tile_copy(c).start()
        for q in range(arows // TILE):
            block = c * (arows // TILE) + q
            a = abuf[pl.ds(pl.multiple_of(block * TILE, TILE), TILE), :]
            top = a.astype(BF16)
            stack[block, 0:TILE, :] = top
            stack[block, TILE : 2 * TILE, :] = (a - top.astype(F32)).astype(BF16)

    slot_copy.wait()

    @pl.loop(0, CHUNKS)
    def _(c):
        tile_copy(c).wait()
        for u in range(trows):
            slot = slots[c * trows + u]
            row = pl.multiple_of((slot // COLS) * TILE, TILE)
            col = slot % COLS
            t = tbuf[c * trows + u]
            top = t.astype(BF16)
            low = (t - top.astype(F32)).astype(BF16)
            part = jnp.dot(jnp.concatenate([top, top], axis=1), stack[col], preferred_element_type=F32)
            part = part + jnp.dot(low, stack[col, 0:TILE, :], preferred_element_type=F32)
            acc[pl.ds(row, TILE), :] += part

    s = row_set(place("y"), place("core"))
    for a in range(32):
        for own in range(2):
            b_high = (a // HALF + s + own) % 2
            row = pl.multiple_of(a * 32 + b_high * HALF, HALF)
            outs[own][pl.ds(a * HALF, HALF), :] = acc[pl.ds(row, HALF), :]


def orders_kernel(unused_ref, turned_ref, place_ref, back_ref):
    s, x = row_set(place("y"), place("core")), place("occ")

    def column(g, transposed):
        occ = x
        for n in range(1, NX):
            occ = jnp.where(g // 64 == n, turn(x, STEPS[n], NX, s), occ)
        outer, inner = (g // EIGHT) % EIGHT, g % EIGHT
        if transposed:
            outer, inner = inner, outer
        return outer * 32 + EIGHT * occ + inner

    down = lax.broadcasted_iota(jnp.int32, (256, 256), 0)
    along = lax.broadcasted_iota(jnp.int32, (256, 256), 1)
    turned_ref[...] = (down == column(along, True)).astype(F32).astype(BF16)
    place_ref[...] = (down == column(along, False)).astype(F32).astype(BF16)
    back_ref[...] = (along == column(down, False)).astype(F32).astype(BF16)


def split_kernel(keep_ref, recv_ref, turned_ref, own_ref, p1_ref, p2_ref, p3_ref, xbuf):
    mirrored = permute_lanes(keep_ref[...] + recv_ref[...], turned_ref[...])
    for t in range(2):
        xbuf[t] = mirrored[:, t * 128 : t * 128 + 128]
    s = row_set(place("y"), place("core"))
    pieces = (own_ref, p1_ref, p2_ref, p3_ref)
    left = lax.broadcasted_iota(jnp.int32, (HALF, 128), 1) < 64
    for a in range(HALF):
        rows = pl.ds(a * HALF, HALF)
        for t in range(2):
            one = xbuf[t, pl.ds(s * 256 + a, HALF, stride=HALF), :]
            two = xbuf[t, pl.ds((1 - s) * 256 + a, HALF, stride=HALF), :]
            pieces[2 * t][rows, :] = jnp.where(left, one, pltpu.roll(two, 64, 1))
            pieces[2 * t + 1][rows, :] = jnp.where(left, pltpu.roll(one, 64, 1), two)


def direct_kernel(keep_ref, recv_ref, place_ref, out_ref):
    out_ref[...] = permute_lanes(keep_ref[...] + recv_ref[...], place_ref[...])


def mirror_kernel(direct_ref, own_ref, q1_ref, q2_ref, q3_ref, o0_ref, o1_ref, o2_ref, o3_ref, total):
    y, core = place("y"), place("core")
    arrived = (own_ref, q1_ref, q2_ref, q3_ref)
    groups = [arrived[STEPS.index((NX - k) % NX)] for k in STEPS]
    left = lax.broadcasted_iota(jnp.int32, (256, 128), 1) < 64
    for t in range(2):
        even, odd = groups[2 * t][...], groups[2 * t + 1][...]
        lanes = pl.ds(t * 128, 128)
        total[0:256, lanes] = direct_ref[0:256, lanes] + jnp.where(left, even, pltpu.roll(odd, 64, 1))
        total[256:512, lanes] = direct_ref[256:512, lanes] + jnp.where(left, pltpu.roll(even, 64, 1), odd)
    for k, ref in zip(YSTEPS, (o0_ref, o1_ref, o2_ref, o3_ref)):
        ref[...] = total[pl.ds(pl.multiple_of(turn(y, k, NY, row_set(y, core)) * 128, 128), 128), :]


def gather_kernel(r0_ref, r1_ref, r2_ref, r3_ref, out_ref):
    for p, z in enumerate(Z_ORDER):
        rows = pl.ds(z * HALF, HALF)
        out_ref[p] = (r0_ref[rows, :] + r1_ref[rows, :]) + (r2_ref[rows, :] + r3_ref[rows, :])


def finish_kernel(parts_ref, denom_ref, back_ref, out_ref):
    acc = parts_ref[0]
    for z in range(1, NZ):
        acc = acc + parts_ref[z]
    out_ref[...] = permute_lanes(acc, back_ref[...]) / denom_ref[...]


def params(mib):
    return pltpu.CompilerParams(vmem_limit_bytes=mib << 20)


def f32(*shape):
    return jax.ShapeDtypeStruct(shape, F32)


def kernel_call(body, name, args, outs, scratch=()):
    single = not isinstance(outs, list)
    return pl.pallas_call(
        body,
        in_specs=[vmem_spec()] * len(args),
        out_specs=vmem_spec() if single else [vmem_spec()] * len(outs),
        out_shape=outs,
        scratch_shapes=[pltpu.VMEM(shape, F32) for shape in scratch],
        compiler_params=params(8),
        name=name,
    )(*args)


def shift_y(k):
    pairs = []
    for y in range(NY):
        for z in range(NZ):
            for core in range(2):
                s = core ^ (y >= NY // 2)
                to = (y + (k if s == 0 else -k)) % NY
                core_to = s ^ (to >= NY // 2)
                pairs.append(((y * NZ + z) * 2 + core, (to * NZ + z) * 2 + core_to))
    return pairs


def shift_x(k):
    pairs = []
    for y in range(NY):
        for core in range(2):
            s = core ^ (y >= NY // 2)
            for x in range(NX):
                to = (x + (k if s == 0 else -k)) % NX
                pairs.append(((y * 2 + core) * NX + x, (y * 2 + core) * NX + to))
    return pairs


def z_groups():
    return [[(y * NZ + z) * 2 + core for z in Z_ORDER] for y in range(NY) for core in range(2)]


def in_hbm(x):
    return pltpu.with_memory_space_constraint(x, pltpu.HBM)


def per_device(tiles, tile_slot, amplitudes, occ_energy, vir_energy):
    y, z, core, x = (place(name) for name in ("y", "z", "core", "occ"))
    keep, send = pl.pallas_call(
        ladder_kernel,
        in_specs=[pl.BlockSpec(memory_space=pltpu.HBM)] * 3,
        out_specs=[vmem_spec()] * 2,
        out_shape=[f32(512, 256)] * 2,
        scratch_shapes=[
            pltpu.SMEM((CAP,), jnp.int32),
            pltpu.VMEM((CAP, TILE, TILE), F32),
            pltpu.VMEM((COLS * TILE, 256), F32),
            pltpu.VMEM((COLS, 2 * TILE, 256), BF16),
            pltpu.VMEM((1024 + TILE, 256), F32),
            pltpu.SemaphoreType.DMA,
            pltpu.SemaphoreType.DMA((CHUNKS,)),
            pltpu.SemaphoreType.DMA((CHUNKS,)),
        ],
        compiler_params=params(24),
        name="ladder",
    )(in_hbm(tile_slot), in_hbm(tiles), in_hbm(amplitudes))
    recv = lax.ppermute(send, "core", [(0, 1), (1, 0)])
    turned, grouped, back = pl.pallas_call(
        orders_kernel,
        in_specs=[pl.BlockSpec(memory_space=pl.ANY)],
        out_specs=[vmem_spec()] * 3,
        out_shape=[jax.ShapeDtypeStruct((256, 256), BF16)] * 3,
        compiler_params=params(8),
        name="orders",
    )(keep)
    pieces = kernel_call(split_kernel, "split", [keep, recv, turned], [f32(256, 128)] * 4, [(2, 512, 128)])
    moved = [lax.ppermute(pieces[n], ("y", "core", "occ"), shift_x(STEPS[n])) for n in range(1, NX)]
    direct = kernel_call(direct_kernel, "direct", [keep, recv, grouped], f32(512, 256))
    own, *others = kernel_call(
        mirror_kernel, "mirror", [direct, pieces[0], *moved], [f32(128, 256)] * 4, [(512, 256)]
    )
    moved = [lax.ppermute(others[n - 1], VIR, shift_y(YSTEPS[n])) for n in range(1, NY)]
    summed = kernel_call(gather_kernel, "gather", [own, *moved], f32(NZ, HALF, 256))
    parts = lax.all_to_all(summed, VIR, 0, 0, axis_index_groups=z_groups())

    def pick(table, index):
        orbital = lax.broadcasted_iota(jnp.int32, (index.shape[0], 32), 1)
        return jnp.sum(jnp.where(index[:, None] == orbital, table[None, :], 0.0), axis=1)

    n = lax.broadcasted_iota(jnp.int32, (256,), 0)
    row = lax.broadcasted_iota(jnp.int32, (HALF,), 0)
    pair = pick(occ_energy, x * 8 + n // 32) + pick(occ_energy, n % 32)
    first = pick(vir_energy, jnp.full((HALF,), y * NZ + z, jnp.int32))
    second = pick(vir_energy, core * HALF + row)
    denominator = pair[None, :] - first[:, None] - second[:, None]
    return kernel_call(finish_kernel, "finish", [parts, denominator, back], f32(HALF, 256))


def solution(mesh):
    fine = Mesh(mesh.devices.reshape(NY, NZ, 2, NX), ("y", "z", "core", "occ"))
    in_specs = (P(VIR, None, None), P(VIR), P(VIR, "occ"), P(), P())
    return jax.shard_map(
        per_device, mesh=fine, in_specs=in_specs, out_specs=P(VIR, "occ"), check_vma=False
    )
```

```python
import functools

import jax
import jax.numpy as jnp
from jax import lax
from jax.experimental import pallas as pl
from jax.experimental.pallas import tpu as pltpu
from jax.sharding import Mesh
from jax.sharding import PartitionSpec as P

F32 = jnp.float32
BF16 = jnp.bfloat16
TILE = 128
CAP = 64
COLS = 32
CHUNKS = 4
NY, NZ, NX = 4, 8, 4
STEPS = (0, 2, 1, 3)
YSTEPS = (0, 2, 3, 1)
HALF = 16
EIGHT = 8
VIR = ("y", "z", "core")
Z_ORDER = (4, 3, 5, 2, 6, 1, 7, 0)


def vmem_spec():
    return pl.BlockSpec(memory_space=pltpu.VMEM)


def split3(x):
    top = x.astype(BF16)
    rest = x - top.astype(F32)
    mid = rest.astype(BF16)
    low = (rest - mid.astype(F32)).astype(BF16)
    return top, mid, low


def permute_lanes(x, place):
    top, mid, low = split3(x)
    out = jnp.dot(low, place, preferred_element_type=F32)
    out = out + jnp.dot(mid, place, preferred_element_type=F32)
    return out + jnp.dot(top, place, preferred_element_type=F32)


def row_set(y, core):
    return lax.bitwise_xor(core, (y >= NY // 2).astype(jnp.int32))


def place(name):
    return lax.axis_index(name).astype(jnp.int32)


def turn(position, k, size, which):
    return lax.rem(position + size + k * (1 - 2 * which), size)


def ladder_kernel(slot_hbm, tiles_hbm, amps_hbm, *rest):
    outs, (slots, tbuf, abuf, stack, acc, ssem, tsem, asem) = rest[:2], rest[2:]
    arows, trows = abuf.shape[0] // CHUNKS, CAP // CHUNKS

    def amp_copy(c):
        rows = pl.ds(c * arows, arows)
        return pltpu.make_async_copy(amps_hbm.at[rows], abuf.at[rows], asem.at[c])

    def tile_copy(c):
        rows = pl.ds(c * trows, trows)
        return pltpu.make_async_copy(tiles_hbm.at[rows], tbuf.at[rows], tsem.at[c])

    slot_copy = pltpu.make_async_copy(slot_hbm, slots, ssem)
    slot_copy.start()
    for c in range(CHUNKS):
        amp_copy(c).start()
    acc[...] = jnp.zeros_like(acc)

    @pl.loop(0, CHUNKS)
    def _(c):
        amp_copy(c).wait()
        tile_copy(c).start()
        for q in range(arows // TILE):
            block = c * (arows // TILE) + q
            a = abuf[pl.ds(pl.multiple_of(block * TILE, TILE), TILE), :]
            top = a.astype(BF16)
            stack[block, 0:TILE, :] = top
            stack[block, TILE : 2 * TILE, :] = (a - top.astype(F32)).astype(BF16)

    slot_copy.wait()

    @pl.loop(0, CHUNKS)
    def _(c):
        tile_copy(c).wait()
        for u in range(trows):
            slot = slots[c * trows + u]
            row = pl.multiple_of((slot // COLS) * TILE, TILE)
            col = slot % COLS
            t = tbuf[c * trows + u]
            top = t.astype(BF16)
            low = (t - top.astype(F32)).astype(BF16)
            part = jnp.dot(jnp.concatenate([top, top], axis=1), stack[col], preferred_element_type=F32)
            part = part + jnp.dot(low, stack[col, 0:TILE, :], preferred_element_type=F32)
            acc[pl.ds(row, TILE), :] += part

    s = row_set(place("y"), place("core"))
    for a in range(32):
        for own in range(2):
            b_high = (a // HALF + s + own) % 2
            row = pl.multiple_of(a * 32 + b_high * HALF, HALF)
            outs[own][pl.ds(a * HALF, HALF), :] = acc[pl.ds(row, HALF), :]


def orders_kernel(unused_ref, turned_ref, place_ref, back_ref):
    s, x = row_set(place("y"), place("core")), place("occ")

    def column(g, transposed):
        occ = x
        for n in range(1, NX):
            occ = jnp.where(g // 64 == n, turn(x, STEPS[n], NX, s), occ)
        outer, inner = (g // EIGHT) % EIGHT, g % EIGHT
        if transposed:
            outer, inner = inner, outer
        return outer * 32 + EIGHT * occ + inner

    down = lax.broadcasted_iota(jnp.int32, (256, 256), 0)
    along = lax.broadcasted_iota(jnp.int32, (256, 256), 1)
    turned_ref[...] = (down == column(along, True)).astype(F32).astype(BF16)
    place_ref[...] = (down == column(along, False)).astype(F32).astype(BF16)
    back_ref[...] = (along == column(down, False)).astype(F32).astype(BF16)


def split_kernel(keep_ref, recv_ref, turned_ref, own_ref, p1_ref, p2_ref, p3_ref, xbuf):
    mirrored = permute_lanes(keep_ref[...] + recv_ref[...], turned_ref[...])
    for t in range(2):
        xbuf[t] = mirrored[:, t * 128 : t * 128 + 128]
    s = row_set(place("y"), place("core"))
    pieces = (own_ref, p1_ref, p2_ref, p3_ref)
    left = lax.broadcasted_iota(jnp.int32, (HALF, 128), 1) < 64
    for a in range(HALF):
        rows = pl.ds(a * HALF, HALF)
        for t in range(2):
            one = xbuf[t, pl.ds(s * 256 + a, HALF, stride=HALF), :]
            two = xbuf[t, pl.ds((1 - s) * 256 + a, HALF, stride=HALF), :]
            pieces[2 * t][rows, :] = jnp.where(left, one, pltpu.roll(two, 64, 1))
            pieces[2 * t + 1][rows, :] = jnp.where(left, pltpu.roll(one, 64, 1), two)


def direct_kernel(keep_ref, recv_ref, place_ref, out_ref):
    out_ref[...] = permute_lanes(keep_ref[...] + recv_ref[...], place_ref[...])


def mirror_kernel(direct_ref, own_ref, q1_ref, q2_ref, q3_ref, o0_ref, o1_ref, o2_ref, o3_ref, total):
    y, core = place("y"), place("core")
    arrived = (own_ref, q1_ref, q2_ref, q3_ref)
    groups = [arrived[STEPS.index((NX - k) % NX)] for k in STEPS]
    left = lax.broadcasted_iota(jnp.int32, (256, 128), 1) < 64
    for t in range(2):
        even, odd = groups[2 * t][...], groups[2 * t + 1][...]
        lanes = pl.ds(t * 128, 128)
        total[0:256, lanes] = direct_ref[0:256, lanes] + jnp.where(left, even, pltpu.roll(odd, 64, 1))
        total[256:512, lanes] = direct_ref[256:512, lanes] + jnp.where(left, pltpu.roll(even, 64, 1), odd)
    for k, ref in zip(YSTEPS, (o0_ref, o1_ref, o2_ref, o3_ref)):
        ref[...] = total[pl.ds(pl.multiple_of(turn(y, k, NY, row_set(y, core)) * 128, 128), 128), :]


def gather_kernel(r0_ref, r1_ref, r2_ref, r3_ref, out_ref):
    for p, z in enumerate(Z_ORDER):
        rows = pl.ds(z * HALF, HALF)
        out_ref[p] = (r0_ref[rows, :] + r1_ref[rows, :]) + (r2_ref[rows, :] + r3_ref[rows, :])


def finish_kernel(parts_ref, denom_ref, back_ref, out_ref):
    acc = parts_ref[0]
    for z in range(1, NZ):
        acc = acc + parts_ref[z]
    out_ref[...] = permute_lanes(acc, back_ref[...]) / denom_ref[...]


def params(mib):
    return pltpu.CompilerParams(vmem_limit_bytes=mib << 20)


def f32(*shape):
    return jax.ShapeDtypeStruct(shape, F32)


def kernel_call(body, name, args, outs, scratch=()):
    single = not isinstance(outs, list)
    return pl.pallas_call(
        body,
        in_specs=[vmem_spec()] * len(args),
        out_specs=vmem_spec() if single else [vmem_spec()] * len(outs),
        out_shape=outs,
        scratch_shapes=[pltpu.VMEM(shape, F32) for shape in scratch],
        compiler_params=params(8),
        name=name,
    )(*args)


def shift_y(k):
    pairs = []
    for y in range(NY):
        for z in range(NZ):
            for core in range(2):
                s = core ^ (y >= NY // 2)
                to = (y + (k if s == 0 else -k)) % NY
                core_to = s ^ (to >= NY // 2)
                pairs.append(((y * NZ + z) * 2 + core, (to * NZ + z) * 2 + core_to))
    return pairs


def shift_x(k):
    pairs = []
    for y in range(NY):
        for core in range(2):
            s = core ^ (y >= NY // 2)
            for x in range(NX):
                to = (x + (k if s == 0 else -k)) % NX
                pairs.append(((y * 2 + core) * NX + x, (y * 2 + core) * NX + to))
    return pairs


def z_groups():
    return [[(y * NZ + z) * 2 + core for z in Z_ORDER] for y in range(NY) for core in range(2)]


def in_hbm(x):
    return pltpu.with_memory_space_constraint(x, pltpu.HBM)


def per_device(tiles, tile_slot, amplitudes, occ_energy, vir_energy):
    y, z, core, x = (place(name) for name in ("y", "z", "core", "occ"))
    keep, send = pl.pallas_call(
        ladder_kernel,
        in_specs=[pl.BlockSpec(memory_space=pltpu.HBM)] * 3,
        out_specs=[vmem_spec()] * 2,
        out_shape=[f32(512, 256)] * 2,
        scratch_shapes=[
            pltpu.SMEM((CAP,), jnp.int32),
            pltpu.VMEM((CAP, TILE, TILE), F32),
            pltpu.VMEM((COLS * TILE, 256), F32),
            pltpu.VMEM((COLS, 2 * TILE, 256), BF16),
            pltpu.VMEM((1024 + TILE, 256), F32),
            pltpu.SemaphoreType.DMA,
            pltpu.SemaphoreType.DMA((CHUNKS,)),
            pltpu.SemaphoreType.DMA((CHUNKS,)),
        ],
        compiler_params=params(24),
        name="ladder",
    )(in_hbm(tile_slot), in_hbm(tiles), in_hbm(amplitudes))
    recv = lax.ppermute(send, "core", [(0, 1), (1, 0)])
    turned, grouped, back = pl.pallas_call(
        orders_kernel,
        in_specs=[pl.BlockSpec(memory_space=pl.ANY)],
        out_specs=[vmem_spec()] * 3,
        out_shape=[jax.ShapeDtypeStruct((256, 256), BF16)] * 3,
        compiler_params=params(8),
        name="orders",
    )(keep)
    pieces = kernel_call(split_kernel, "split", [keep, recv, turned], [f32(256, 128)] * 4, [(2, 512, 128)])
    moved = [lax.ppermute(pieces[n], ("y", "core", "occ"), shift_x(STEPS[n])) for n in range(1, NX)]
    direct = kernel_call(direct_kernel, "direct", [keep, recv, grouped], f32(512, 256))
    own, *others = kernel_call(
        mirror_kernel, "mirror", [direct, pieces[0], *moved], [f32(128, 256)] * 4, [(512, 256)]
    )
    moved = [lax.ppermute(others[n - 1], VIR, shift_y(YSTEPS[n])) for n in range(1, NY)]
    summed = kernel_call(gather_kernel, "gather", [own, *moved], f32(NZ, HALF, 256))
    parts = lax.all_to_all(summed, VIR, 0, 0, axis_index_groups=z_groups())

    def pick(table, index):
        orbital = lax.broadcasted_iota(jnp.int32, (index.shape[0], 32), 1)
        return jnp.sum(jnp.where(index[:, None] == orbital, table[None, :], 0.0), axis=1)

    n = lax.broadcasted_iota(jnp.int32, (256,), 0)
    row = lax.broadcasted_iota(jnp.int32, (HALF,), 0)
    pair = pick(occ_energy, x * 8 + n // 32) + pick(occ_energy, n % 32)
    first = pick(vir_energy, jnp.full((HALF,), y * NZ + z, jnp.int32))
    second = pick(vir_energy, core * HALF + row)
    denominator = pair[None, :] - first[:, None] - second[:, None]
    return kernel_call(finish_kernel, "finish", [parts, denominator, back], f32(HALF, 256))


def solution(mesh):
    fine = Mesh(mesh.devices.reshape(NY, NZ, 2, NX), ("y", "z", "core", "occ"))
    in_specs = (P(VIR, None, None), P(VIR), P(VIR, "occ"), P(), P())
    return jax.shard_map(
        per_device, mesh=fine, in_specs=in_specs, out_specs=P(VIR, "occ"), check_vma=False
    )
```

```python
import functools

import jax
import jax.numpy as jnp
from jax import lax
from jax.experimental import pallas as pl
from jax.experimental.pallas import tpu as pltpu
from jax.sharding import Mesh
from jax.sharding import PartitionSpec as P

F32 = jnp.float32
BF16 = jnp.bfloat16
TILE = 128
CAP = 64
COLS = 32
CHUNKS = 4
NY, NZ, NX = 4, 8, 4
STEPS = (0, 2, 1, 3)
YSTEPS = (0, 2, 3, 1)
HALF = 16
EIGHT = 8
VIR = ("y", "z", "core")
Z_ORDER = (4, 3, 5, 2, 6, 1, 7, 0)


def vmem_spec():
    return pl.BlockSpec(memory_space=pltpu.VMEM)


def split3(x):
    top = x.astype(BF16)
    rest = x - top.astype(F32)
    mid = rest.astype(BF16)
    low = (rest - mid.astype(F32)).astype(BF16)
    return top, mid, low


def permute_lanes(x, place):
    top, mid, low = split3(x)
    out = jnp.dot(low, place, preferred_element_type=F32)
    out = out + jnp.dot(mid, place, preferred_element_type=F32)
    return out + jnp.dot(top, place, preferred_element_type=F32)


def row_set(y, core):
    return lax.bitwise_xor(core, (y >= NY // 2).astype(jnp.int32))


def place(name):
    return lax.axis_index(name).astype(jnp.int32)


def turn(position, k, size, which):
    return lax.rem(position + size + k * (1 - 2 * which), size)


def ladder_kernel(slot_hbm, tiles_hbm, amps_hbm, *rest):
    outs, (slots, tbuf, abuf, stack, acc, ssem, tsem, asem) = rest[:2], rest[2:]
    arows, trows = abuf.shape[0] // CHUNKS, CAP // CHUNKS

    def amp_copy(c):
        rows = pl.ds(c * arows, arows)
        return pltpu.make_async_copy(amps_hbm.at[rows], abuf.at[rows], asem.at[c])

    def tile_copy(c):
        rows = pl.ds(c * trows, trows)
        return pltpu.make_async_copy(tiles_hbm.at[rows], tbuf.at[rows], tsem.at[c])

    slot_copy = pltpu.make_async_copy(slot_hbm, slots, ssem)
    slot_copy.start()
    for c in range(CHUNKS):
        amp_copy(c).start()
    acc[...] = jnp.zeros_like(acc)

    @pl.loop(0, CHUNKS)
    def _(c):
        amp_copy(c).wait()
        tile_copy(c).start()
        for q in range(arows // TILE):
            block = c * (arows // TILE) + q
            a = abuf[pl.ds(pl.multiple_of(block * TILE, TILE), TILE), :]
            top = a.astype(BF16)
            stack[block, 0:TILE, :] = top
            stack[block, TILE : 2 * TILE, :] = (a - top.astype(F32)).astype(BF16)

    slot_copy.wait()

    @pl.loop(0, CHUNKS)
    def _(c):
        tile_copy(c).wait()
        for u in range(trows):
            slot = slots[c * trows + u]
            row = pl.multiple_of((slot // COLS) * TILE, TILE)
            col = slot % COLS
            t = tbuf[c * trows + u]
            top = t.astype(BF16)
            low = (t - top.astype(F32)).astype(BF16)
            part = jnp.dot(jnp.concatenate([top, top], axis=1), stack[col], preferred_element_type=F32)
            part = part + jnp.dot(low, stack[col, 0:TILE, :], preferred_element_type=F32)
            acc[pl.ds(row, TILE), :] += part

    s = row_set(place("y"), place("core"))
    for a in range(32):
        for own in range(2):
            b_high = (a // HALF + s + own) % 2
            row = pl.multiple_of(a * 32 + b_high * HALF, HALF)
            outs[own][pl.ds(a * HALF, HALF), :] = acc[pl.ds(row, HALF), :]


def orders_kernel(unused_ref, turned_ref, place_ref, back_ref):
    s, x = row_set(place("y"), place("core")), place("occ")

    def column(g, transposed):
        occ = x
        for n in range(1, NX):
            occ = jnp.where(g // 64 == n, turn(x, STEPS[n], NX, s), occ)
        outer, inner = (g // EIGHT) % EIGHT, g % EIGHT
        if transposed:
            outer, inner = inner, outer
        return outer * 32 + EIGHT * occ + inner

    down = lax.broadcasted_iota(jnp.int32, (256, 256), 0)
    along = lax.broadcasted_iota(jnp.int32, (256, 256), 1)
    turned_ref[...] = (down == column(along, True)).astype(F32).astype(BF16)
    place_ref[...] = (down == column(along, False)).astype(F32).astype(BF16)
    back_ref[...] = (along == column(down, False)).astype(F32).astype(BF16)


def split_kernel(keep_ref, recv_ref, turned_ref, own_ref, p1_ref, p2_ref, p3_ref, xbuf):
    mirrored = permute_lanes(keep_ref[...] + recv_ref[...], turned_ref[...])
    for t in range(2):
        xbuf[t] = mirrored[:, t * 128 : t * 128 + 128]
    s = row_set(place("y"), place("core"))
    pieces = (own_ref, p1_ref, p2_ref, p3_ref)
    left = lax.broadcasted_iota(jnp.int32, (HALF, 128), 1) < 64
    for a in range(HALF):
        rows = pl.ds(a * HALF, HALF)
        for t in range(2):
            one = xbuf[t, pl.ds(s * 256 + a, HALF, stride=HALF), :]
            two = xbuf[t, pl.ds((1 - s) * 256 + a, HALF, stride=HALF), :]
            pieces[2 * t][rows, :] = jnp.where(left, one, pltpu.roll(two, 64, 1))
            pieces[2 * t + 1][rows, :] = jnp.where(left, pltpu.roll(one, 64, 1), two)


def direct_kernel(keep_ref, recv_ref, place_ref, out_ref):
    out_ref[...] = permute_lanes(keep_ref[...] + recv_ref[...], place_ref[...])


def mirror_kernel(direct_ref, own_ref, q1_ref, q2_ref, q3_ref, o0_ref, o1_ref, o2_ref, o3_ref, total):
    y, core = place("y"), place("core")
    arrived = (own_ref, q1_ref, q2_ref, q3_ref)
    groups = [arrived[STEPS.index((NX - k) % NX)] for k in STEPS]
    left = lax.broadcasted_iota(jnp.int32, (256, 128), 1) < 64
    for t in range(2):
        even, odd = groups[2 * t][...], groups[2 * t + 1][...]
        lanes = pl.ds(t * 128, 128)
        total[0:256, lanes] = direct_ref[0:256, lanes] + jnp.where(left, even, pltpu.roll(odd, 64, 1))
        total[256:512, lanes] = direct_ref[256:512, lanes] + jnp.where(left, pltpu.roll(even, 64, 1), odd)
    for k, ref in zip(YSTEPS, (o0_ref, o1_ref, o2_ref, o3_ref)):
        ref[...] = total[pl.ds(pl.multiple_of(turn(y, k, NY, row_set(y, core)) * 128, 128), 128), :]


def gather_kernel(r0_ref, r1_ref, r2_ref, r3_ref, out_ref):
    for p, z in enumerate(Z_ORDER):
        rows = pl.ds(z * HALF, HALF)
        out_ref[p] = (r0_ref[rows, :] + r1_ref[rows, :]) + (r2_ref[rows, :] + r3_ref[rows, :])


def finish_kernel(parts_ref, denom_ref, back_ref, out_ref):
    acc = parts_ref[0]
    for z in range(1, NZ):
        acc = acc + parts_ref[z]
    top, mid, low = split3(acc)
    terms = jnp.dot(jnp.concatenate([low, mid, top], axis=0), back_ref[...], preferred_element_type=F32)
    total = (terms[0:HALF] + terms[HALF : 2 * HALF]) + terms[2 * HALF : 3 * HALF]
    out_ref[...] = total / denom_ref[...]


def params(mib):
    return pltpu.CompilerParams(vmem_limit_bytes=mib << 20)


def f32(*shape):
    return jax.ShapeDtypeStruct(shape, F32)


def kernel_call(body, name, args, outs, scratch=()):
    single = not isinstance(outs, list)
    return pl.pallas_call(
        body,
        in_specs=[vmem_spec()] * len(args),
        out_specs=vmem_spec() if single else [vmem_spec()] * len(outs),
        out_shape=outs,
        scratch_shapes=[pltpu.VMEM(shape, F32) for shape in scratch],
        compiler_params=params(8),
        name=name,
    )(*args)


def shift_y(k):
    pairs = []
    for y in range(NY):
        for z in range(NZ):
            for core in range(2):
                s = core ^ (y >= NY // 2)
                to = (y + (k if s == 0 else -k)) % NY
                core_to = s ^ (to >= NY // 2)
                pairs.append(((y * NZ + z) * 2 + core, (to * NZ + z) * 2 + core_to))
    return pairs


def shift_x(k):
    pairs = []
    for y in range(NY):
        for core in range(2):
            s = core ^ (y >= NY // 2)
            for x in range(NX):
                to = (x + (k if s == 0 else -k)) % NX
                pairs.append(((y * 2 + core) * NX + x, (y * 2 + core) * NX + to))
    return pairs


def z_groups():
    return [[(y * NZ + z) * 2 + core for z in Z_ORDER] for y in range(NY) for core in range(2)]


def in_hbm(x):
    return pltpu.with_memory_space_constraint(x, pltpu.HBM)


def per_device(tiles, tile_slot, amplitudes, occ_energy, vir_energy):
    y, z, core, x = (place(name) for name in ("y", "z", "core", "occ"))
    keep, send = pl.pallas_call(
        ladder_kernel,
        in_specs=[pl.BlockSpec(memory_space=pltpu.HBM)] * 3,
        out_specs=[vmem_spec()] * 2,
        out_shape=[f32(512, 256)] * 2,
        scratch_shapes=[
            pltpu.SMEM((CAP,), jnp.int32),
            pltpu.VMEM((CAP, TILE, TILE), F32),
            pltpu.VMEM((COLS * TILE, 256), F32),
            pltpu.VMEM((COLS, 2 * TILE, 256), BF16),
            pltpu.VMEM((1024 + TILE, 256), F32),
            pltpu.SemaphoreType.DMA,
            pltpu.SemaphoreType.DMA((CHUNKS,)),
            pltpu.SemaphoreType.DMA((CHUNKS,)),
        ],
        compiler_params=params(24),
        name="ladder",
    )(in_hbm(tile_slot), in_hbm(tiles), in_hbm(amplitudes))
    recv = lax.ppermute(send, "core", [(0, 1), (1, 0)])
    turned, grouped, back = pl.pallas_call(
        orders_kernel,
        in_specs=[pl.BlockSpec(memory_space=pl.ANY)],
        out_specs=[vmem_spec()] * 3,
        out_shape=[jax.ShapeDtypeStruct((256, 256), BF16)] * 3,
        compiler_params=params(8),
        name="orders",
    )(keep)
    pieces = kernel_call(split_kernel, "split", [keep, recv, turned], [f32(256, 128)] * 4, [(2, 512, 128)])
    moved = [lax.ppermute(pieces[n], ("y", "core", "occ"), shift_x(STEPS[n])) for n in range(1, NX)]
    direct = kernel_call(direct_kernel, "direct", [keep, recv, grouped], f32(512, 256))
    own, *others = kernel_call(
        mirror_kernel, "mirror", [direct, pieces[0], *moved], [f32(128, 256)] * 4, [(512, 256)]
    )
    moved = [lax.ppermute(others[n - 1], VIR, shift_y(YSTEPS[n])) for n in range(1, NY)]
    summed = kernel_call(gather_kernel, "gather", [own, *moved], f32(NZ, HALF, 256))
    parts = lax.all_to_all(summed, VIR, 0, 0, axis_index_groups=z_groups())

    def pick(table, index):
        orbital = lax.broadcasted_iota(jnp.int32, (index.shape[0], 32), 1)
        return jnp.sum(jnp.where(index[:, None] == orbital, table[None, :], 0.0), axis=1)

    n = lax.broadcasted_iota(jnp.int32, (256,), 0)
    row = lax.broadcasted_iota(jnp.int32, (HALF,), 0)
    pair = pick(occ_energy, x * 8 + n // 32) + pick(occ_energy, n % 32)
    first = pick(vir_energy, jnp.full((HALF,), y * NZ + z, jnp.int32))
    second = pick(vir_energy, core * HALF + row)
    denominator = pair[None, :] - first[:, None] - second[:, None]
    return kernel_call(finish_kernel, "finish", [parts, denominator, back], f32(HALF, 256))


def solution(mesh):
    fine = Mesh(mesh.devices.reshape(NY, NZ, 2, NX), ("y", "z", "core", "occ"))
    in_specs = (P(VIR, None, None), P(VIR), P(VIR, "occ"), P(), P())
    return jax.shard_map(
        per_device, mesh=fine, in_specs=in_specs, out_specs=P(VIR, "occ"), check_vma=False
    )
```
